512 devices in a mesh: ktot: 32 (over z_lo, y, core), kvir: 16 (over z_hi, x).
Axes of the slice: x: 4, y: 4, z: 16 (z_hi: 4, z_lo: 4; z = z_hi * 4 + z_lo), core: 2. Of those that a mesh axis runs over, the one named last changes fastest.
Arguments:
- amplitudes: bfloat16 [32, 16, 672, 1024], P('ktot', 'kvir'), may hold values from -6 to 6
- ladder_integrals: bfloat16 [32, 16, 1024, 1024], P('ktot', 'kvir'), may hold values from -0.046875 to 0.046875
- listed: int32 [32, 16], P('ktot', 'kvir'), may hold values 0 or 1
- current: bfloat16 [32, 672, 1024], P('ktot', 'kvir'), may hold values from -3 to 3
- denominators: float32 [32, 672, 1024], P('ktot', 'kvir'), may hold values from 2 to 8
- cycle_integrals: bfloat16 [32, 512, 512], P('ktot', 'kvir'), may hold values from -0.25 to 0.25
Outputs:
- ladder_res: bfloat16 [32, 672, 1024], P('ktot', 'kvir')
- cycle_res: float32 [32, 1344, 1344], P('ktot', 'kvir')
The draws below stay inside these ranges and needn't reach their ends.
All inputs are finite; a program needn't handle non-finite values. No bound on the sum of `listed` on one device may be relied on, other than what follows from the above.
Results may differ from the reference program's by a relative error of at most 0.017.
Values may be sent and summed in bfloat16 or wider, within the bound.
No kernel may reach another device: no remote copies, remote signals or barrier semaphores. Data moves between devices by JAX's collectives and lax.ppermute only.
A program may use at most 64 MiB of HBM per device.

```python
import math
import jax
import jax.numpy as jnp
from jax import lax

VV = 1024
ROWS = 672
NKT = 32
NKC = 16
CYCLE = 512
YR = 1344
N_KTOT = 32
N_KVIR = 16


def with_ends(drawn, stream_key, least, top_value):
    spot = [jax.random.randint(jax.random.fold_in(stream_key, axis), (), 0, length) for axis, length in enumerate(drawn.shape)]
    main_axis = drawn.shape.index(max(drawn.shape))
    beside = spot[:main_axis] + [(spot[main_axis] + 1) % drawn.shape[main_axis]] + spot[main_axis + 1:]
    return drawn.at[tuple(spot)].set(least).at[tuple(beside)].set(top_value)


def steps_of(stream_key, extent, shards, smallest, top_value):
    gain, own = 1.0, jax.random.fold_in(stream_key, 6)
    for position, shards_of in shards:
        heights = jnp.exp(jax.random.uniform(jax.random.fold_in(own, position), (shards_of,), jnp.float32, smallest / len(shards), top_value / len(shards)))
        gain = gain * jnp.repeat(heights, extent[position] // shards_of).reshape([-1 if axis == position else 1 for axis in range(len(extent))])
    return gain


def normal_values(rng, extent, deviation, limit, shards=(), held_as=jnp.bfloat16):
    result = jax.random.normal(rng, extent, jnp.float32) * deviation
    if len(shards) > 0:
        result = steps_of(rng, extent, shards, -0.22, 0.18) * result
    return jnp.clip(result, min=-limit, max=limit).astype(held_as)


def setup_inputs(seed: int = 0) -> dict:
    arg_keys = jax.random.split(jax.random.key(seed), 7)
    return {
        "amplitudes": normal_values(arg_keys[0], (NKT, NKC, ROWS, VV), 1.0, 6.0, ((0, 32), (1, 16))),
        "ladder_integrals": normal_values(arg_keys[1], (NKT, NKC, VV, VV), (VV * NKC) ** -0.5, 0.046875, ((0, 32), (1, 16))),
        "listed": with_ends((jax.random.randint(arg_keys[2], (NKT, NKC), 0, 4) < 3).astype(jnp.int32), jax.random.fold_in(arg_keys[2], 1), 0, 1),
        "current": normal_values(arg_keys[3], (NKT, ROWS, VV), 0.5, 3.0, ((0, 32), (1, 16))),
        "denominators": jnp.clip(jnp.exp(math.log(8.0) - 1.3862944 * jax.random.uniform(arg_keys[4], (NKT, ROWS, VV), jnp.float32) ** steps_of(arg_keys[4], (NKT, ROWS, VV), ((0, 32), (1, 16)), -0.2, 0.2)), 2.0, 8.0),
        "cycle_integrals": normal_values(arg_keys[5], (NKT, CYCLE, CYCLE), CYCLE ** -0.5, 0.25, ((0, 32), (1, 16))),
    }


def reference(amplitudes, ladder_integrals, listed, current, denominators, cycle_integrals):
    def per_total(inputs):
        amp_blocks, int_blocks, marks = inputs

        def per_contracted(running, item):
            amp_one, int_one, mark_one = item
            product = jnp.dot(amp_one, int_one, preferred_element_type=jnp.float32)
            return running + product * mark_one.astype(jnp.float32), None

        summed, unused = lax.scan(per_contracted, jnp.zeros((ROWS, VV), jnp.float32), (amp_blocks, int_blocks, marks))
        return summed

    ladder = lax.map(per_total, (amplitudes, ladder_integrals, listed))
    ladder_res = ladder.astype(jnp.bfloat16)
    updated = (current.astype(jnp.float32) + ladder / denominators).astype(jnp.bfloat16)
    row_share = ROWS // N_KVIR
    col_width = VV // N_KTOT
    cycle_matrix = updated.reshape(NKT, N_KVIR, row_share, NKT, col_width)
    cycle_matrix = cycle_matrix.transpose(3, 2, 0, 1, 4).reshape(NKT, YR, CYCLE)

    def per_transfer(inputs):
        cycle_block, cycle_weights = inputs
        column_parts = cycle_block.reshape(YR, N_KVIR, col_width).transpose(1, 0, 2)
        weight_parts = cycle_weights.reshape(N_KVIR, col_width, CYCLE)

        def add_part(running, item):
            column_one, weight_one = item
            partial_sum = jnp.dot(column_one, weight_one, preferred_element_type=jnp.float32)
            rounded = lax.optimization_barrier(partial_sum.astype(jnp.bfloat16))
            return running + rounded.astype(jnp.float32), None

        summed, unused = lax.scan(add_part, jnp.zeros((YR, CYCLE), jnp.float32), (column_parts, weight_parts))
        mixed = summed.astype(jnp.bfloat16)
        return jnp.dot(mixed, cycle_block.T, preferred_element_type=jnp.float32) * (CYCLE ** -0.5)

    cycle_res = lax.map(per_transfer, (cycle_matrix, cycle_integrals))
    return ladder_res, cycle_res
```

```python
import jax
import jax.numpy as jnp
from jax import lax
from jax.sharding import Mesh, PartitionSpec as P

KTOT = ("zl", "y", "core")
KVIR = ("zh", "x")
SIZES = (4, 4, 2, 4, 4)


def exchange(blocks, axis):
    return lax.all_to_all(blocks, axis, split_axis=0, concat_axis=0, tiled=True)


def steps(block, axis):
    count = lax.axis_size(axis)
    pieces = [block]
    for step in range(1, count):
        ring = [(i, (i + step) % count) for i in range(count)]
        pieces.append(lax.ppermute(block, axis, ring))
    return pieces


def ordered(pieces, axis):
    count = len(pieces)
    me = lax.axis_index(axis)
    stacked = jnp.stack(pieces)
    return jnp.stack([lax.dynamic_index_in_dim(stacked, (me - p) % count, 0, False) for p in range(count)])


def spread(block, axis):
    return ordered(steps(block, axis), axis)


def shards(amplitudes, ladder_integrals, listed, current, denominators, cycle_integrals):
    amp_block = amplitudes[0, 0]
    weights = ladder_integrals[0, 0]
    mark = listed[0, 0].astype(jnp.float32)
    nx = lax.axis_size("x")
    nz = lax.axis_size("zh")
    rows = amp_block.shape[0]
    width = amp_block.shape[1]
    rows_dev = current.shape[1]
    tot_count = lax.axis_size(KTOT)
    col_width = width // tot_count

    own = cycle_integrals[0]
    cols = own.shape[1]
    own = own.reshape(col_width, nz, nx, col_width).transpose(0, 2, 1, 3).reshape(col_width, cols)
    ints = spread(own, "zh").reshape(nz * col_width, cols)
    int_pieces = steps(ints, "x")

    by_x = amp_block.reshape(nz, nx, rows_dev, width).transpose(1, 0, 2, 3).reshape(rows, width)
    part = (jnp.dot(by_x, weights, preferred_element_type=jnp.float32) * mark).astype(jnp.bfloat16)
    got = exchange(part, "x").reshape(nx, nz * rows_dev, width)
    part = got.astype(jnp.float32).sum(0).astype(jnp.bfloat16)
    got = exchange(part.reshape(nz, rows_dev, width), "zh")
    ladder = got.astype(jnp.float32).sum(0)
    updated = (current[0].astype(jnp.float32) + ladder / denominators[0]).astype(jnp.bfloat16)

    received = lax.all_to_all(
        updated.reshape(rows_dev, tot_count, col_width), KTOT, split_axis=1, concat_axis=1, tiled=True
    )
    local = received.transpose(2, 0, 1).reshape(col_width, rows_dev * tot_count)
    cycle = lax.all_gather(local, "zh", axis=0).reshape(nz * col_width, -1)
    cycle_rows = cycle.shape[1]
    share = cycle_rows // (nx * nz)
    start = lax.axis_index(KVIR) * share
    first = (((0,), (0,)), ((), ()))
    pieces = steps(cycle, "x")
    mixed = 0.0
    for piece, weight in zip(pieces, int_pieces):
        mine = lax.dynamic_slice_in_dim(piece, start, share, 1)
        mixed += lax.dot_general(mine, weight, first, preferred_element_type=jnp.float32)
    mixed = mixed.astype(jnp.bfloat16)
    out = 0.0
    wide = nz * col_width
    me = lax.axis_index("x")
    for step, piece in enumerate(pieces):
        left = lax.dynamic_slice_in_dim(mixed, ((me - step) % nx) * wide, wide, 1)
        out += jnp.dot(left, piece, preferred_element_type=jnp.float32)
    return (ladder.astype(jnp.bfloat16)[None], (out * cols ** (-0.5))[None])


def solution(mesh):
    fine = Mesh(mesh.devices.reshape(SIZES), KTOT + KVIR)
    block = P(KTOT, KVIR, None)
    return jax.shard_map(
        shards,
        mesh=fine,
        in_specs=(
            P(KTOT, KVIR, None, None),
            P(KTOT, KVIR, None, None),
            P(KTOT, KVIR),
            block,
            block,
            block,
        ),
        out_specs=(block, block),
        check_vma=False,
    )
```

```python
import jax
import jax.numpy as jnp
from jax import lax
from jax.experimental import pallas as pl
from jax.experimental.pallas import tpu as pltpu
from jax.sharding import Mesh, PartitionSpec as P


KTOT = ("zl", "y", "core")
KVIR = ("zh", "x")
SIZES = (4, 4, 2, 4, 4)
INTERPRET = False
BLOCK = 512
WHOLE = pl.BlockSpec(memory_space=pltpu.VMEM)


def near(array):
    return array if INTERPRET else pltpu.with_memory_space_constraint(array, pltpu.VMEM)


def near_out(shape):
    return jax.ShapeDtypeStruct(shape, jnp.bfloat16) if INTERPRET else pltpu.VMEM(shape, jnp.bfloat16)


def exchange(blocks, axis):
    return lax.all_to_all(blocks, axis, split_axis=0, concat_axis=0, tiled=True)


def steps(block, axis):
    count = lax.axis_size(axis)
    pieces = [block]
    for step in range(1, count):
        ring = [(i, (i + step) % count) for i in range(count)]
        pieces.append(lax.ppermute(block, axis, ring))
    return pieces


def ordered(pieces, axis):
    count = len(pieces)
    me = lax.axis_index(axis)
    stacked = jnp.stack(pieces)
    return jnp.stack([lax.dynamic_index_in_dim(stacked, (me - p) % count, 0, False) for p in range(count)])


def columns_block(width):
    return BLOCK if width % BLOCK == 0 else width


def ladder_part(amp, weights, listed, nz, nx):
    rows, inner = amp.shape
    width = weights.shape[1]
    one = rows // (nz * nx)
    tn = columns_block(width)

    def kernel(mark_ref, amp_ref, w_ref, out_ref):
        product = jnp.dot(amp_ref[...], w_ref[...], preferred_element_type=jnp.float32)
        product = product * mark_ref[...].astype(jnp.float32)
        here = pl.ds(pl.multiple_of(pl.program_id(0) * tn, tn), tn)
        for x in range(nx):
            slabs = [product[(z * nx + x) * one : (z * nx + x + 1) * one] for z in range(nz)]
            out_ref[x, :, here] = jnp.concatenate(slabs, 0).astype(jnp.bfloat16)

    return pl.pallas_call(
        kernel,
        grid=(width // tn,),
        in_specs=[
            pl.BlockSpec((1, 1), lambda j: (0, 0)),
            pl.BlockSpec((rows, inner), lambda j: (0, 0)),
            pl.BlockSpec((inner, tn), lambda j: (0, j)),
        ],
        out_specs=WHOLE,
        out_shape=near_out((nx, nz * one, width)),
        interpret=INTERPRET,
        name="ladder_part",
    )(listed, amp, weights)


def sum_over_x(got, nz):
    nx, rows, width = got.shape
    one = rows // nz
    tn = columns_block(width)

    def kernel(in_ref, out_ref):
        for j in range(width // tn):
            here = slice(j * tn, (j + 1) * tn)
            total = in_ref[0, :, here].astype(jnp.float32)
            for x in range(1, nx):
                total = total + in_ref[x, :, here].astype(jnp.float32)
            for z in range(nz):
                out_ref[z, :, here] = total[z * one : (z + 1) * one].astype(jnp.bfloat16)

    return pl.pallas_call(
        kernel,
        in_specs=[WHOLE],
        out_specs=WHOLE,
        out_shape=near_out((nz, one, width)),
        interpret=INTERPRET,
        name="sum_over_x",
    )(near(got))


def update(got, current, denominators):
    nz, one, width = got.shape

    def kernel(in_ref, current_ref, den_ref, ladder_ref, updated_ref):
        total = in_ref[0].astype(jnp.float32)
        for z in range(1, nz):
            total = total + in_ref[z].astype(jnp.float32)
        ladder_ref[...] = total.astype(jnp.bfloat16)
        updated_ref[...] = (current_ref[...].astype(jnp.float32) + total / den_ref[...]).astype(jnp.bfloat16)

    return pl.pallas_call(
        kernel,
        in_specs=[WHOLE] * 3,
        out_specs=[WHOLE] * 2,
        out_shape=[jax.ShapeDtypeStruct((one, width), jnp.bfloat16), near_out((one, width))],
        interpret=INTERPRET,
        name="update",
    )(near(got), current, denominators)


def step(amplitudes, ladder_integrals, listed, current, denominators, cycle_integrals):
    nx = lax.axis_size("x")
    nz = lax.axis_size("zh")
    rows_dev, width = current.shape[1:]
    tot_count = lax.axis_size(KTOT)
    col_width = width // tot_count

    cols = cycle_integrals.shape[2]

    part = ladder_part(amplitudes[0, 0], ladder_integrals[0, 0], listed, nz, nx)
    part, own = lax.optimization_barrier((part, cycle_integrals[0]))
    got = exchange(part, "x")
    own = own.reshape(col_width, nz, nx, col_width).transpose(0, 2, 1, 3).reshape(col_width, cols)
    own_pieces = steps(own, "zh")
    part = sum_over_x(got, nz)
    got = exchange(part, "zh")
    ints = ordered(own_pieces, "zh").reshape(nz * col_width, cols)
    int_pieces = steps(ints, "x")
    ladder, updated = update(got, current[0], denominators[0])

    received = lax.all_to_all(
        updated.reshape(rows_dev, tot_count, col_width), KTOT, split_axis=1, concat_axis=1, tiled=True
    )
    local = received.transpose(2, 0, 1).reshape(col_width, rows_dev * tot_count)
    cycle = lax.all_gather(local, "zh", axis=0).reshape(nz * col_width, -1)
    cycle_rows = cycle.shape[1]
    share = cycle_rows // (nx * nz)
    start = lax.axis_index(KVIR) * share
    first = (((0,), (0,)), ((), ()))
    pieces = steps(cycle, "x")
    mixed = 0.0
    for piece, weight in zip(pieces, int_pieces):
        mine = lax.dynamic_slice_in_dim(piece, start, share, 1)
        mixed += lax.dot_general(mine, weight, first, preferred_element_type=jnp.float32)
    mixed = mixed.astype(jnp.bfloat16)
    out = 0.0
    wide = nz * col_width
    me = lax.axis_index("x")
    for step, piece in enumerate(pieces):
        left = lax.dynamic_slice_in_dim(mixed, ((me - step) % nx) * wide, wide, 1)
        out += jnp.dot(left, piece, preferred_element_type=jnp.float32)
    return (ladder[None], (out * cols ** (-0.5))[None])


def solution(mesh):
    fine = Mesh(mesh.devices.reshape(SIZES), KTOT + KVIR)
    block = P(KTOT, KVIR, None)
    return jax.shard_map(
        step,
        mesh=fine,
        in_specs=(
            P(KTOT, KVIR, None, None),
            P(KTOT, KVIR, None, None),
            P(KTOT, KVIR),
            block,
            block,
            block,
        ),
        out_specs=(block, block),
        check_vma=False,
    )
```

```python
import jax
import jax.numpy as jnp
from jax import lax
from jax.experimental import pallas as pl
from jax.experimental.pallas import tpu as pltpu
from jax.sharding import Mesh, PartitionSpec as P


KTOT = ("zl", "y", "core")
KVIR = ("zh", "x")
SIZES = (4, 4, 2, 4, 4)
INTERPRET = False
BLOCK = 512
WHOLE = pl.BlockSpec(memory_space=pltpu.VMEM)


def near(array):
    return array if INTERPRET else pltpu.with_memory_space_constraint(array, pltpu.VMEM)


def near_out(shape):
    return jax.ShapeDtypeStruct(shape, jnp.bfloat16) if INTERPRET else pltpu.VMEM(shape, jnp.bfloat16)


def exchange(blocks, axis):
    return lax.all_to_all(blocks, axis, split_axis=0, concat_axis=0, tiled=True)


def steps(block, axis):
    count = lax.axis_size(axis)
    pieces = [block]
    for step in range(1, count):
        ring = [(i, (i + step) % count) for i in range(count)]
        pieces.append(lax.ppermute(block, axis, ring))
    return pieces


def ordered(pieces, axis):
    count = len(pieces)
    me = lax.axis_index(axis)
    stacked = jnp.stack(pieces)
    return jnp.stack([lax.dynamic_index_in_dim(stacked, (me - p) % count, 0, False) for p in range(count)])


def columns_block(width):
    return BLOCK if width % BLOCK == 0 else width


def ladder_part(amp, weights, listed, nz, nx):
    rows, inner = amp.shape
    width = weights.shape[1]
    one = rows // (nz * nx)
    tn = columns_block(width)

    def kernel(mark_ref, amp_ref, w_ref, out_ref):
        product = jnp.dot(amp_ref[...], w_ref[...], preferred_element_type=jnp.float32)
        product = product * mark_ref[0, 0].astype(jnp.float32)
        here = pl.ds(pl.multiple_of(pl.program_id(0) * tn, tn), tn)
        for x in range(nx):
            slabs = [product[(z * nx + x) * one : (z * nx + x + 1) * one] for z in range(nz)]
            out_ref[x, :, here] = jnp.concatenate(slabs, 0).astype(jnp.bfloat16)

    return pl.pallas_call(
        kernel,
        grid=(width // tn,),
        in_specs=[
            pl.BlockSpec(memory_space=pltpu.SMEM),
            pl.BlockSpec((rows, inner), lambda j: (0, 0)),
            pl.BlockSpec((inner, tn), lambda j: (0, j)),
        ],
        out_specs=WHOLE,
        out_shape=near_out((nx, nz * one, width)),
        interpret=INTERPRET,
        name="ladder_part",
    )(listed, amp, weights)


def sum_over_x(got, nz, me):
    nx, rows, width = got.shape
    one = rows // nz
    tn = columns_block(width)

    def kernel(me_ref, in_ref, *refs):
        out_refs, slabs = refs[:-1], refs[-1]
        for j in range(width // tn):
            here = slice(j * tn, (j + 1) * tn)
            total = in_ref[0, :, here].astype(jnp.float32)
            for x in range(1, nx):
                total = total + in_ref[x, :, here].astype(jnp.float32)
            for z in range(nz):
                slabs[z, :, here] = total[z * one : (z + 1) * one].astype(jnp.bfloat16)
        for s, out_ref in enumerate(out_refs):
            out_ref[...] = slabs[lax.rem(me_ref[0] + s, nz)]

    return pl.pallas_call(
        kernel,
        in_specs=[pl.BlockSpec(memory_space=pltpu.SMEM), WHOLE],
        out_specs=[WHOLE] * nz,
        out_shape=[near_out((one, width))] * nz,
        scratch_shapes=[pltpu.VMEM((nz, one, width), jnp.bfloat16)],
        interpret=INTERPRET,
        name="sum_over_x",
    )(me.reshape(1), near(got))


def update(parts, current, denominators):
    one, width = current.shape

    def kernel(*refs):
        in_refs, (current_ref, den_ref, ladder_ref, updated_ref) = refs[:-4], refs[-4:]
        total = in_refs[0][...].astype(jnp.float32)
        for in_ref in in_refs[1:]:
            total = total + in_ref[...].astype(jnp.float32)
        ladder_ref[...] = total.astype(jnp.bfloat16)
        updated_ref[...] = (current_ref[...].astype(jnp.float32) + total / den_ref[...]).astype(jnp.bfloat16)

    return pl.pallas_call(
        kernel,
        in_specs=[WHOLE] * (len(parts) + 2),
        out_specs=[WHOLE] * 2,
        out_shape=[near_out((one, width))] * 2,
        interpret=INTERPRET,
        name="update",
    )(*map(near, (*parts, current, denominators)))


def step(amplitudes, ladder_integrals, listed, current, denominators, cycle_integrals):
    nx = lax.axis_size("x")
    nz = lax.axis_size("zh")
    rows_dev, width = current.shape[1:]
    tot_count = lax.axis_size(KTOT)
    col_width = width // tot_count

    cols = cycle_integrals.shape[2]

    part = ladder_part(amplitudes[0, 0], ladder_integrals[0, 0], listed, nz, nx)
    part, own = lax.optimization_barrier((part, cycle_integrals[0]))
    got = exchange(part, "x")
    own = own.reshape(col_width, nz, nx, col_width).transpose(0, 2, 1, 3).reshape(col_width, cols)
    own_pieces = steps(own, "zh")
    parts = sum_over_x(got, nz, lax.axis_index("zh"))
    got = [parts[0]]
    for step in range(1, nz):
        ring = [(i, (i + step) % nz) for i in range(nz)]
        got.append(lax.ppermute(parts[step], "zh", ring))
    ints = ordered(own_pieces, "zh").reshape(nz * col_width, cols)
    int_pieces = steps(ints, "x")
    ladder, updated = update(got, current[0], denominators[0])

    received = lax.all_to_all(
        updated.reshape(rows_dev, tot_count, col_width), KTOT, split_axis=1, concat_axis=1, tiled=True
    )
    local = received.transpose(2, 0, 1).reshape(col_width, rows_dev * tot_count)
    cycle = lax.all_gather(local, "zh", axis=0).reshape(nz * col_width, -1)
    cycle_rows = cycle.shape[1]
    share = cycle_rows // (nx * nz)
    start = lax.axis_index(KVIR) * share
    first = (((0,), (0,)), ((), ()))
    pieces = steps(cycle, "x")
    mixed = 0.0
    for piece, weight in zip(pieces, int_pieces):
        mine = lax.dynamic_slice_in_dim(piece, start, share, 1)
        mixed += lax.dot_general(mine, weight, first, preferred_element_type=jnp.float32)
    mixed = mixed.astype(jnp.bfloat16)
    out = 0.0
    wide = nz * col_width
    me = lax.axis_index("x")
    for step, piece in enumerate(pieces):
        left = lax.dynamic_slice_in_dim(mixed, ((me - step) % nx) * wide, wide, 1)
        out += jnp.dot(left, piece, preferred_element_type=jnp.float32)
    return (ladder[None], (out * cols ** (-0.5))[None])


def solution(mesh):
    fine = Mesh(mesh.devices.reshape(SIZES), KTOT + KVIR)
    block = P(KTOT, KVIR, None)
    return jax.shard_map(
        step,
        mesh=fine,
        in_specs=(
            P(KTOT, KVIR, None, None),
            P(KTOT, KVIR, None, None),
            P(KTOT, KVIR),
            block,
            block,
            block,
        ),
        out_specs=(block, block),
        check_vma=False,
    )
```

```python
import jax
import jax.numpy as jnp
from jax import lax
from jax.experimental import pallas as pl
from jax.experimental.pallas import tpu as pltpu
from jax.sharding import Mesh, PartitionSpec as P


KTOT = ("zl", "y", "core")
KVIR = ("zh", "x")
SIZES = (4, 4, 2, 4, 4)
INTERPRET = False
BLOCK = 512
WHOLE = pl.BlockSpec(memory_space=pltpu.VMEM)
HBM = pltpu.HBM


def near(array):
    return array if INTERPRET else pltpu.with_memory_space_constraint(array, pltpu.VMEM)


def near_out(shape):
    return jax.ShapeDtypeStruct(shape, jnp.bfloat16) if INTERPRET else pltpu.VMEM(shape, jnp.bfloat16)


def exchange(blocks, axis):
    return lax.all_to_all(blocks, axis, split_axis=0, concat_axis=0, tiled=True)


def steps(block, axis):
    count = lax.axis_size(axis)
    pieces = [block]
    for step in range(1, count):
        ring = [(i, (i + step) % count) for i in range(count)]
        pieces.append(lax.ppermute(block, axis, ring))
    return pieces


def send(parts, axis):
    count = lax.axis_size(axis)
    got = [parts[0]]
    for step in range(1, count):
        ring = [(i, (i + step) % count) for i in range(count)]
        got.append(lax.ppermute(parts[step], axis, ring))
    return got


def columns_block(width):
    return BLOCK if width % BLOCK == 0 else width


def ladder_part(amp, weights, listed, nz, nx, me):
    rows, inner = amp.shape
    width = weights.shape[1]
    one = rows // (nz * nx)
    tn = columns_block(width)

    def kernel(me_ref, listed_ref, amp_ref, w_ref, *refs):
        out_refs, (mark_ref, arrived) = refs[:-2], refs[-2:]
        fetch = pltpu.make_async_copy(listed_ref, mark_ref, arrived)

        @pl.when(pl.program_id(0) == 0)
        def _():
            fetch.start()

        product = jnp.dot(amp_ref[...], w_ref[...], preferred_element_type=jnp.float32)

        @pl.when(pl.program_id(0) == 0)
        def _():
            fetch.wait()

        product = product * mark_ref[0, 0].astype(jnp.float32)
        here = pl.ds(pl.multiple_of(pl.program_id(0) * tn, tn), tn)
        for mine in range(nx):

            @pl.when(me_ref[0] == mine)
            def _():
                for s, out_ref in enumerate(out_refs):
                    x = (mine + s) % nx
                    slabs = [product[(z * nx + x) * one : (z * nx + x + 1) * one] for z in range(nz)]
                    out_ref[:, here] = jnp.concatenate(slabs, 0).astype(jnp.bfloat16)

    return pl.pallas_call(
        kernel,
        grid=(width // tn,),
        in_specs=[
            pl.BlockSpec(memory_space=pltpu.SMEM),
            pl.BlockSpec(memory_space=HBM),
            pl.BlockSpec((rows, inner), lambda j: (0, 0)),
            pl.BlockSpec((inner, tn), lambda j: (0, j)),
        ],
        out_specs=[WHOLE] * nx,
        out_shape=[near_out((nz * one, width))] * nx,
        scratch_shapes=[pltpu.SMEM((1, 1), jnp.int32), pltpu.SemaphoreType.DMA],
        interpret=INTERPRET,
        name="ladder_part",
    )(me.reshape(1), listed, amp, weights)


def sum_over_x(parts, nz, me):
    rows, width = parts[0].shape
    one = rows // nz
    tn = columns_block(width)

    def kernel(me_ref, *refs):
        in_refs, out_refs, slabs = refs[: len(parts)], refs[len(parts) : -1], refs[-1]
        for j in range(width // tn):
            here = slice(j * tn, (j + 1) * tn)
            total = in_refs[0][:, here].astype(jnp.float32)
            for in_ref in in_refs[1:]:
                total = total + in_ref[:, here].astype(jnp.float32)
            for z in range(nz):
                slabs[z, :, here] = total[z * one : (z + 1) * one].astype(jnp.bfloat16)
        for s, out_ref in enumerate(out_refs):
            out_ref[...] = slabs[lax.rem(me_ref[0] + s, nz)]

    return pl.pallas_call(
        kernel,
        in_specs=[pl.BlockSpec(memory_space=pltpu.SMEM)] + [WHOLE] * len(parts),
        out_specs=[WHOLE] * nz,
        out_shape=[near_out((one, width))] * nz,
        scratch_shapes=[pltpu.VMEM((nz, one, width), jnp.bfloat16)],
        interpret=INTERPRET,
        name="sum_over_x",
    )(me.reshape(1), *map(near, parts))


def update(parts, current, denominators):
    one, width = current.shape

    def kernel(*refs):
        in_refs, (current_ref, den_ref, ladder_ref, updated_ref) = refs[:-4], refs[-4:]
        total = in_refs[0][...].astype(jnp.float32)
        for in_ref in in_refs[1:]:
            total = total + in_ref[...].astype(jnp.float32)
        ladder_ref[...] = total.astype(jnp.bfloat16)
        updated_ref[...] = (current_ref[...].astype(jnp.float32) + total / den_ref[...]).astype(jnp.bfloat16)

    return pl.pallas_call(
        kernel,
        in_specs=[WHOLE] * (len(parts) + 2),
        out_specs=[WHOLE] * 2,
        out_shape=[near_out((one, width))] * 2,
        interpret=INTERPRET,
        name="update",
    )(*map(near, (*parts, current, denominators)))


def step(amplitudes, ladder_integrals, listed, current, denominators, cycle_integrals):
    nx = lax.axis_size("x")
    nz = lax.axis_size("zh")
    rows_dev, width = current.shape[1:]
    tot_count = lax.axis_size(KTOT)
    col_width = width // tot_count

    cols = cycle_integrals.shape[2]

    parts = ladder_part(amplitudes[0, 0], ladder_integrals[0, 0], listed, nz, nx, lax.axis_index("x"))
    parts, own = lax.optimization_barrier((parts, cycle_integrals[0]))
    got = send(parts, "x")
    ints = exchange(jnp.broadcast_to(own[None], (nz, col_width, cols)), "zh")
    parts = sum_over_x(got, nz, lax.axis_index("zh"))
    got = send(parts, "zh")
    ints = ints.reshape(nz * col_width, nz, nx, col_width).transpose(0, 2, 1, 3).reshape(nz * col_width, cols)
    int_pieces = steps(ints, "x")
    ladder, updated = update(got, current[0], denominators[0])

    received = lax.all_to_all(
        updated.reshape(rows_dev, tot_count, col_width), KTOT, split_axis=1, concat_axis=1, tiled=True
    )
    local = received.transpose(2, 0, 1).reshape(col_width, rows_dev * tot_count)
    cycle = lax.all_gather(local, "zh", axis=0).reshape(nz * col_width, -1)
    cycle_rows = cycle.shape[1]
    share = cycle_rows // (nx * nz)
    start = lax.axis_index(KVIR) * share
    first = (((0,), (0,)), ((), ()))
    pieces = steps(cycle, "x")
    mixed = 0.0
    for piece, weight in zip(pieces, int_pieces):
        mine = lax.dynamic_slice_in_dim(piece, start, share, 1)
        mixed += lax.dot_general(mine, weight, first, preferred_element_type=jnp.float32)
    mixed = mixed.astype(jnp.bfloat16)
    out = 0.0
    wide = nz * col_width
    me = lax.axis_index("x")
    for step, piece in enumerate(pieces):
        left = lax.dynamic_slice_in_dim(mixed, ((me - step) % nx) * wide, wide, 1)
        out += jnp.dot(left, piece, preferred_element_type=jnp.float32)
    return (ladder[None], (out * cols ** (-0.5))[None])


def solution(mesh):
    fine = Mesh(mesh.devices.reshape(SIZES), KTOT + KVIR)
    block = P(KTOT, KVIR, None)
    return jax.shard_map(
        step,
        mesh=fine,
        in_specs=(
            P(KTOT, KVIR, None, None),
            P(KTOT, KVIR, None, None),
            P(KTOT, KVIR),
            block,
            block,
            block,
        ),
        out_specs=(block, block),
        check_vma=False,
    )
```
